32 devices in a mesh: sample: 4 (over x, core), space: 8 (over z, y).
Axes of the slice: x: 2, y: 2, z: 4, core: 2. Of those that a mesh axis runs over, the one named last changes fastest.
Arguments:
- acts: bfloat16 [8, 8, 16, 8, 8, 128], P('sample', 'space'), may hold values from -6 to 6
- weight: float32 [3456, 128], P('space'), may hold values from -0.109375 to 0.109375
- moment: float32 [3456, 128], P('space'), may hold values from -3 to 3
- second: float32 [3456, 128], P('space'), may hold values from 0.05 to 2
- cotangent: bfloat16 [8, 8, 16, 8, 8, 128], P('sample', 'space'), may hold values from -6 to 6
Outputs:
- output: bfloat16 [8, 8, 16, 8, 8, 128], P('sample', 'space')
- input_grad: bfloat16 [8, 8, 16, 8, 8, 128], P('sample', 'space')
- weight_grad: float32 [3456, 128], P('space')
- new_weight: float32 [3456, 128], P('space')
- new_moment: float32 [3456, 128], P('space')
- new_second: float32 [3456, 128], P('space')
The draws below stay inside these ranges and needn't reach their ends.
All inputs are finite; a program needn't handle non-finite values.
Results may differ from the reference program's by a relative error of at most 0.0062.
Values may be sent and summed in bfloat16 or wider, within the bound.
A program may use at most 64 MiB of HBM per device.

```python
import math
import jax
import jax.numpy as jnp
from jax import lax

CH = 128
BX = 16
BY = 8
BZ = 8
GY = 2
GZ = 4
BRICKS = 8
BATCH = 8


def block_scale(rng, extent, pieces, low, high):
    factor_of = 1.0
    for position, shards_of in pieces:
        draws = jax.random.uniform(jax.random.fold_in(jax.random.fold_in(rng, 6), position), (shards_of,), jnp.float32, low / len(pieces), high / len(pieces))
        factor_of = factor_of * jnp.repeat(jnp.exp(draws), extent[position] // shards_of).reshape((-1,) + (1,) * (len(extent) - 1 - position))
    return factor_of


def noise(own_key, dims, width, most, cuts=(), dtype=jnp.bfloat16):
    array = jax.random.normal(own_key, dims, jnp.float32) * width
    if len(cuts) > 0:
        array = block_scale(own_key, dims, cuts, -0.22, 0.18) * array
    return jnp.clip(array, min=-most, max=most).astype(dtype)


def setup_inputs(seed: int = 0) -> dict:
    key_of = jax.random.split(jax.random.key(seed), 6)
    acts = noise(key_of[0], (BATCH, BRICKS, BX, BY, BZ, CH), 1.0, 6.0, ((0, 4), (1, 8)))
    weight = noise(key_of[1], (27 * CH, CH), (27 * CH) ** -0.5, 0.109375, ((0, 8),), jnp.float32)
    moment = noise(key_of[2], (27 * CH, CH), 0.5, 3.0, ((0, 8),), jnp.float32)
    second = jnp.clip(jnp.exp(math.log(2.0) - 3.6888794 * jax.random.uniform(key_of[3], (27 * CH, CH), jnp.float32) ** block_scale(key_of[3], (27 * CH, CH), ((0, 8),), -0.2, 0.2)), 0.05, 2.0)
    cotangent = noise(key_of[4], (BATCH, BRICKS, BX, BY, BZ, CH), 1.0, 6.0, ((0, 4), (1, 8)))
    return {"acts": acts, "weight": weight, "moment": moment, "second": second, "cotangent": cotangent}


root_coef = 0.7978845608
cubic_coef = 0.044715

def to_crop(field):
    nb, nr, sx, sy, sz, nc = field.shape
    groups = nr // (GY * GZ)
    shaped = field.reshape(nb, groups, GY, GZ, sx, sy, sz, nc)
    shaped = shaped.transpose(0, 1, 4, 2, 5, 3, 6, 7)
    return shaped.reshape(nb, groups * sx, GY * sy, GZ * sz, nc)

def to_bricks(field):
    nb, nx, ny, nz, nc = field.shape
    groups = nx // BX
    shaped = field.reshape(nb, groups, BX, GY, BY, GZ, BZ, nc)
    shaped = shaped.transpose(0, 1, 3, 5, 2, 4, 6, 7)
    return shaped.reshape(nb, groups * GY * GZ, BX, BY, BZ, nc)

def convolve(field, kernel, padding):
    return lax.conv_general_dilated(field, kernel, (1, 1, 1), padding, dimension_numbers=('NDHWC', 'DHWIO', 'NDHWC'), preferred_element_type=jnp.float32)

def activate(pre):
    inner = root_coef * (pre + cubic_coef * pre * pre * pre)
    tval = jnp.tanh(inner)
    value = 0.5 * pre * (1.0 + tval)
    slope = 0.5 * (1.0 + tval) + 0.5 * pre * (1.0 - tval * tval) * root_coef * (1.0 + 3.0 * cubic_coef * pre * pre)
    return (value, slope)

def kernel_terms(padded, grad_pre):
    nx, ny, nz = (grad_pre.shape[1], grad_pre.shape[2], grad_pre.shape[3])
    terms = []
    for kx in range(3):
        for ky in range(3):
            for kz in range(3):
                window = padded[:, kx:kx + nx, ky:ky + ny, kz:kz + nz, :]
                terms.append(lax.dot_general(window, grad_pre, (((0, 1, 2, 3), (0, 1, 2, 3)), ((), ())), preferred_element_type=jnp.float32))
    stacked = jnp.stack(terms, 0)
    return stacked.reshape(27 * stacked.shape[1], stacked.shape[2])

def adam(weight, moment, second, grad):
    new_moment = 0.9 * moment + 0.1 * grad
    new_second = 0.999 * second + 0.001 * grad * grad
    first_fix = 1.0 - 0.9 ** 10
    second_fix = 1.0 - 0.999 ** 10
    new_weight = weight - 0.001 * (new_moment / first_fix) / (jnp.sqrt(new_second / second_fix) + 1e-08)
    return (new_weight, new_moment, new_second)

def reference(acts, weight, moment, second, cotangent):
    crop = to_crop(acts)
    grad_out = to_crop(cotangent)
    channels = weight.shape[1]
    kernel = weight.astype(jnp.bfloat16).reshape(3, 3, 3, channels, channels)
    pad = [(1, 1), (1, 1), (1, 1)]
    pre = convolve(crop, kernel, pad)
    value, slope = activate(pre)
    output = value.astype(jnp.bfloat16)
    grad_pre = (grad_out.astype(jnp.float32) * slope).astype(jnp.bfloat16)
    flipped = jnp.flip(kernel, (0, 1, 2)).transpose(0, 1, 2, 4, 3)
    input_grad = convolve(grad_pre, flipped, pad).astype(jnp.bfloat16)
    padded = jnp.pad(crop, ((0, 0), (1, 1), (1, 1), (1, 1), (0, 0)))
    total = crop.shape[0] * crop.shape[1] * crop.shape[2] * crop.shape[3]
    weight_grad = kernel_terms(padded, grad_pre) * float(total) ** (-0.5)
    new_weight, new_moment, new_second = adam(weight, moment, second, weight_grad)
    return (to_bricks(output), to_bricks(input_grad), weight_grad, new_weight, new_moment, new_second)
```

```python
import functools

import jax
import jax.numpy as jnp
from jax import lax
from jax.experimental import pallas as pl
from jax.experimental.pallas import tpu as pltpu
from jax.sharding import PartitionSpec as P

GY = 2
GZ = 4
MESH = pl.DeviceIdType.MESH
VM = pl.BlockSpec(memory_space=pltpu.VMEM)

root_coef = 0.7978845608
cubic_coef = 0.044715

SIDES = (1, -1)
DIRS = [(0, 1), (0, -1), (1, 0), (-1, 0)] + [(dy, dz) for dy in SIDES for dz in SIDES]


def shifted(value, axis, by):
    devices = lax.axis_size(axis)
    pairs = [(i, i + by) for i in range(devices) if 0 <= i + by < devices]
    return lax.ppermute(value, axis, pairs)


def convolve(field, kernel):
    return lax.conv_general_dilated(
        field,
        kernel,
        (1, 1, 1),
        "VALID",
        dimension_numbers=("NDHWC", "DHWIO", "NDHWC"),
        preferred_element_type=jnp.float32,
    )


def activate(pre):
    inner = root_coef * (pre + cubic_coef * pre * pre * pre)
    tval = jnp.tanh(inner)
    value = 0.5 * pre * (1.0 + tval)
    slope = 0.5 * (1.0 + tval) + 0.5 * pre * (1.0 - tval * tval) * root_coef * (
        1.0 + 3.0 * cubic_coef * pre * pre
    )
    return (value, slope)


def extend_x(field):
    groups = lax.axis_size("space") // (GY * GZ)
    if groups == 1:
        return jnp.pad(field, ((0, 0), (1, 1), (0, 0), (0, 0), (0, 0)))
    coord = lax.axis_index("space") // (GZ * GY)
    length = field.shape[1]
    below = shifted(field[:, length - 1 : length], "space", GY * GZ)
    above = shifted(field[:, :1], "space", -GY * GZ)
    below = jnp.where(coord > 0, below, jnp.zeros_like(below))
    above = jnp.where(coord < groups - 1, above, jnp.zeros_like(above))
    return jnp.concatenate([below, field, above], 1)


def faces(field):
    ends = {1: field.shape[2] - 1, -1: 0}
    endz = {1: field.shape[3] - 1, -1: 0}
    zf = jnp.stack([field[:, :, :, endz[d], :] for d in SIDES])
    yf = jnp.stack([field[:, :, ends[d], :, :] for d in SIDES])
    cf = jnp.stack([field[:, :, ends[dy], endz[dz], :] for dy in SIDES for dz in SIDES])
    return (zf, yf, cf)


def assemble(field, zf, yf, cf):
    mid = jnp.concatenate([zf[0][:, :, :, None], field, zf[1][:, :, :, None]], 3)
    rows = []
    for i in range(2):
        low, high = cf[2 * i][:, :, None, :], cf[2 * i + 1][:, :, None, :]
        rows.append(jnp.concatenate([low, yf[i], high], 2)[:, :, None])
    return jnp.concatenate([rows[0], mid, rows[1]], 2)


class Halo:
    def __init__(self, ins, outs, send, recv):
        me = lax.axis_index("space")
        self.me, self.send, self.recv = me, send, recv
        self.cz, self.cy = lax.rem(me, GZ), lax.rem(me // GZ, GY)
        self.src = [ins[k // 2].at[k % 2] if k < 4 else ins[2].at[k - 4] for k in range(8)]
        self.dst = [outs[k // 2].at[k % 2] if k < 4 else outs[2].at[k - 4] for k in range(8)]

    def has(self, dy, dz):
        y, z = self.cy + dy, self.cz + dz
        return (y >= 0) & (y < GY) & (z >= 0) & (z < GZ)

    def copy(self, k, to):
        return pltpu.make_async_remote_copy(
            src_ref=self.src[k],
            dst_ref=self.dst[k],
            send_sem=self.send.at[k],
            recv_sem=self.recv.at[k],
            device_id={"space": to},
            device_id_type=MESH,
        )

    def start(self):
        for k, (dy, dz) in enumerate(DIRS):

            @pl.when(self.has(dy, dz))
            def _():
                self.copy(k, self.me + dy * GZ + dz).start()

            @pl.when(jnp.logical_not(self.has(-dy, -dz)))
            def _():
                self.dst[k][...] = jnp.zeros(self.dst[k].shape, self.dst[k].dtype)

    def finish(self):
        for k, (dy, dz) in enumerate(DIRS):

            @pl.when(self.has(-dy, -dz))
            def _():
                self.copy(k, self.me).wait_recv()

            @pl.when(self.has(dy, dz))
            def _():
                self.copy(k, self.me).wait_send()


def greet(n, me, sample):
    barrier = pltpu.get_barrier_semaphore()

    def space_peer(d, _):
        pl.semaphore_signal(barrier, 1, device_id={"space": lax.rem(me + d, n)}, device_id_type=MESH)
        return 0

    lax.fori_loop(1, n, space_peer, 0)
    for d in range(1, 4):
        pl.semaphore_signal(barrier, 1, device_id={"sample": lax.rem(sample + d, 4)}, device_id_type=MESH)
    pl.semaphore_wait(barrier, n + 2)


def remote(src, dst, send, recv, **to):
    return pltpu.make_async_remote_copy(
        src_ref=src, dst_ref=dst, send_sem=send, recv_sem=recv, device_id=to, device_id_type=MESH
    )


LAG = 1


def gather_kernel(n, w, zi, yi, ci, out, zo, yo, co, hs, hr, as_, ar, bs, br, cs, cr):
    me, sample = lax.axis_index("space"), lax.axis_index("sample")
    core, x = lax.rem(sample, 2), sample // 2
    across, partner = (1 - x) * 2 + core, x * 2 + 1 - core
    greet(n, me, sample)
    halo = Halo((zi, yi, ci), (zo, yo, co), hs, hr)
    halo.start()

    def first(d, _):
        o = lax.rem(me + d, n)
        remote(w.at[core, x], out.at[me, core, x], as_.at[o], ar.at[me], space=o).start()
        return 0

    lax.fori_loop(1, n, first, 0)
    out[me] = w[...]

    def rest(t, _):
        @pl.when(t < n)
        def _():
            j = lax.rem(me - t + n, n)
            slot = out.at[j, core, x]
            remote(slot, slot, as_.at[j], ar.at[j], space=me).wait_recv()
            remote(slot, slot, bs.at[j], br.at[j], sample=across).start()

        @pl.when(t > LAG)
        def _():
            j = lax.rem(me - t + LAG + n, n)
            slot = out.at[j, core, 1 - x]
            remote(slot, slot, bs.at[j], br.at[j], sample=across).wait_recv()
            pair = out.at[j, core]
            remote(pair, pair, cs.at[j], cr.at[j], sample=partner).start()

        return 0

    lax.fori_loop(1, n + LAG, rest, 0)

    def last(d, _):
        o = lax.rem(me + d, n)
        pair = out.at[o, 1 - core]
        remote(pair, pair, cs.at[o], cr.at[o], sample=partner).wait_recv()
        remote(w.at[core, x], out.at[me, core, x], as_.at[o], ar.at[me], space=o).wait_send()
        slot = out.at[o, core, x]
        remote(slot, slot, bs.at[o], br.at[o], sample=across).wait_send()
        mine = out.at[o, core]
        remote(mine, mine, cs.at[o], cr.at[o], sample=partner).wait_send()
        return 0

    lax.fori_loop(1, n, last, 0)
    halo.finish()


def reduce_kernel(n, g, zi, yi, ci, out, zo, yo, co, r1, s2, r2, s3, r3, hs, hr, as_, ar, bs, br, cs, cr, ds, dr):
    me, sample = lax.axis_index("space"), lax.axis_index("sample")
    core, x = lax.rem(sample, 2), sample // 2
    across, partner = (1 - x) * 2 + core, x * 2 + 1 - core
    f32, bf16 = jnp.float32, jnp.bfloat16
    greet(n, me, sample)
    halo = Halo((zi, yi, ci), (zo, yo, co), hs, hr)
    halo.start()

    def owner(d):
        return lax.rem(me + 1 + d, n)

    def copy1(o):
        return remote(g.at[o, 1 - core], r1.at[o], as_.at[o], ar.at[o], sample=partner)

    def copy2(o):
        return remote(s2.at[o, 1 - x], r2.at[o], bs.at[o], br.at[o], sample=across)

    def copy3(o):
        return remote(s3.at[o], r3.at[me], cs.at[o], cr.at[me], space=o)

    def first(d, _):
        copy1(owner(d)).start()
        return 0

    lax.fori_loop(0, n, first, 0)

    def rest(t, _):
        @pl.when(t < n)
        def _():
            o = owner(t)
            copy1(o).wait_recv()
            s2[o] = (g[o, core].astype(f32) + r1[o].astype(f32)).astype(bf16)
            copy2(o).start()

        @pl.when(t >= LAG)
        def _():
            o = owner(t - LAG)
            copy2(o).wait_recv()
            s3[o] = (s2[o, x].astype(f32) + r2[o].astype(f32)).astype(bf16)

            @pl.when(t < n + LAG - 1)
            def _():
                copy3(o).start()

        return 0

    lax.fori_loop(0, n + LAG, rest, 0)

    def gather(d, total):
        j = lax.rem(me + n - d, n)
        remote(s3.at[j], r3.at[j], cs.at[j], cr.at[j], space=j).wait_recv()
        return total + r3[j].astype(f32)

    out[core, x] = lax.fori_loop(1, n, gather, s3[me].astype(f32))

    def copy4(d):
        mine = out.at[core, x]
        return remote(mine, mine, ds.at[d], dr.at[d], sample=lax.rem(sample + 1 + d, 4))

    for d in range(3):
        copy4(d).start()
    for d in range(3):
        copy4(d).wait()

    def drain(d, _):
        o = owner(d)
        copy1(o).wait_send()
        copy2(o).wait_send()

        @pl.when(d < n - 1)
        def _():
            copy3(o).wait_send()

        return 0

    lax.fori_loop(0, n, drain, 0)
    halo.finish()


def quarters(value, lead):
    rows = value.shape[-2]
    q = -(-rows // 4)
    if rows != 4 * q:
        value = jnp.pad(value, [(0, 0)] * (value.ndim - 2) + [(0, 4 * q - rows), (0, 0)])
    return value.reshape(*lead, 2, 2, q, value.shape[-1])


def whole_rows(value, rows):
    lead = value.shape[:-4]
    return value.reshape(*lead, -1, value.shape[-1])[..., :rows, :]


def like(arrays):
    return [jax.ShapeDtypeStruct(a.shape, a.dtype) for a in arrays]


def sems(*counts):
    return [pltpu.SemaphoreType.DMA((c,)) for c in counts]


def gather_weights(rows_bf, field):
    n = lax.axis_size("space")
    halo = faces(field)
    w = quarters(rows_bf, ())
    whole, zf, yf, cf = pl.pallas_call(
        functools.partial(gather_kernel, n),
        name="gather_and_halo",
        out_shape=[jax.ShapeDtypeStruct((n, *w.shape), w.dtype), *like(halo)],
        in_specs=[VM] * 4,
        out_specs=[VM] * 4,
        scratch_shapes=sems(8, 8, n, n, n, n, n, n),
        compiler_params=pltpu.CompilerParams(collective_id=0, has_side_effects=True),
    )(w, *halo)
    whole = whole_rows(whole, rows_bf.shape[0]).reshape(-1, rows_bf.shape[1])
    return whole, assemble(field, zf, yf, cf)


def reduce_grads(terms, rows, field):
    n = lax.axis_size("space")
    halo = faces(field)
    channels = terms.shape[-1]
    g = quarters(terms.reshape(n, rows, channels), (n,)).astype(jnp.bfloat16)
    q = g.shape[3]
    bf16 = jnp.bfloat16
    total, zf, yf, cf = pl.pallas_call(
        functools.partial(reduce_kernel, n),
        name="reduce_and_halo",
        out_shape=[jax.ShapeDtypeStruct((2, 2, q, channels), jnp.float32), *like(halo)],
        in_specs=[VM] * 4,
        out_specs=[VM] * 4,
        scratch_shapes=[
            pltpu.VMEM((n, 2, q, channels), bf16),
            pltpu.VMEM((n, 2, q, channels), bf16),
            pltpu.VMEM((n, q, channels), bf16),
            pltpu.VMEM((n, q, channels), bf16),
            pltpu.VMEM((n, q, channels), bf16),
            *sems(8, 8, n, n, n, n, n, n, 3, 3),
        ],
        compiler_params=pltpu.CompilerParams(collective_id=1, has_side_effects=True),
    )(g, *halo)
    return whole_rows(total, rows), assemble(field, zf, yf, cf)


def kernel_terms(padded, grad_pre):
    nx, ny, nz = (grad_pre.shape[1], grad_pre.shape[2], grad_pre.shape[3])
    terms = []
    for kx in range(3):
        for ky in range(3):
            for kz in range(3):
                window = padded[:, kx : kx + nx, ky : ky + ny, kz : kz + nz, :]
                terms.append(
                    lax.dot_general(
                        window,
                        grad_pre,
                        (((0, 1, 2, 3), (0, 1, 2, 3)), ((), ())),
                        preferred_element_type=jnp.float32,
                    )
                )
    stacked = jnp.stack(terms, 0)
    return stacked.reshape(27 * stacked.shape[1], stacked.shape[2])


def local(acts, weight, moment, second, cotangent):
    field = acts[:, 0]
    grad_out = cotangent[:, 0]
    channels = weight.shape[1]
    rows_bf = weight.astype(jnp.bfloat16)
    whole, padded = gather_weights(rows_bf, extend_x(field))
    kernel = whole.reshape(3, 3, 3, channels, channels)
    pre = convolve(padded, kernel)
    value, slope = activate(pre)
    output = value.astype(jnp.bfloat16)
    grad_pre = (grad_out.astype(jnp.float32) * slope).astype(jnp.bfloat16)
    flipped = jnp.flip(kernel, (0, 1, 2)).transpose(0, 1, 2, 4, 3)
    total = (
        field.shape[0]
        * lax.axis_size("sample")
        * lax.axis_size("space")
        * field.shape[1]
        * field.shape[2]
        * field.shape[3]
    )
    local_terms = kernel_terms(padded, grad_pre)
    summed, grad_padded = reduce_grads(local_terms, weight.shape[0], extend_x(grad_pre))
    input_grad = convolve(grad_padded, flipped).astype(jnp.bfloat16)
    weight_grad = summed * float(total) ** (-0.5)
    new_moment = 0.9 * moment + 0.1 * weight_grad
    new_second = 0.999 * second + 0.001 * weight_grad * weight_grad
    first_fix = 1.0 - 0.9**10
    second_fix = 1.0 - 0.999**10
    new_weight = weight - 0.001 * (new_moment / first_fix) / (
        jnp.sqrt(new_second / second_fix) + 1e-08
    )
    return (output[:, None], input_grad[:, None], weight_grad, new_weight, new_moment, new_second)


def solution(mesh):
    in_specs = (
        P("sample", "space", None, None, None, None),
        P("space", None),
        P("space", None),
        P("space", None),
        P("sample", "space", None, None, None, None),
    )
    out_specs = (
        P("sample", "space", None, None, None, None),
        P("sample", "space", None, None, None, None),
        P("space", None),
        P("space", None),
        P("space", None),
        P("space", None),
    )
    return jax.shard_map(local, mesh=mesh, in_specs=in_specs, out_specs=out_specs, check_vma=False)
```

```python
import functools

import jax
import jax.numpy as jnp
from jax import lax
from jax.experimental import pallas as pl
from jax.experimental.pallas import tpu as pltpu
from jax.sharding import PartitionSpec as P

GY = 2
GZ = 4
MESH = pl.DeviceIdType.MESH
VM = pl.BlockSpec(memory_space=pltpu.VMEM)

root_coef = 0.7978845608
cubic_coef = 0.044715

SIDES = (1, -1)
DIRS = [(0, 1), (0, -1), (1, 0), (-1, 0)] + [(dy, dz) for dy in SIDES for dz in SIDES]


def shifted(value, axis, by):
    devices = lax.axis_size(axis)
    pairs = [(i, i + by) for i in range(devices) if 0 <= i + by < devices]
    return lax.ppermute(value, axis, pairs)


def convolve(field, kernel):
    return lax.conv_general_dilated(
        field,
        kernel,
        (1, 1, 1),
        "VALID",
        dimension_numbers=("NDHWC", "DHWIO", "NDHWC"),
        preferred_element_type=jnp.float32,
    )


def activate(pre):
    inner = root_coef * (pre + cubic_coef * pre * pre * pre)
    tval = jnp.tanh(inner)
    value = 0.5 * pre * (1.0 + tval)
    slope = 0.5 * (1.0 + tval) + 0.5 * pre * (1.0 - tval * tval) * root_coef * (
        1.0 + 3.0 * cubic_coef * pre * pre
    )
    return (value, slope)


def extend_x(field):
    groups = lax.axis_size("space") // (GY * GZ)
    if groups == 1:
        return jnp.pad(field, ((0, 0), (1, 1), (0, 0), (0, 0), (0, 0)))
    coord = lax.axis_index("space") // (GZ * GY)
    length = field.shape[1]
    below = shifted(field[:, length - 1 : length], "space", GY * GZ)
    above = shifted(field[:, :1], "space", -GY * GZ)
    below = jnp.where(coord > 0, below, jnp.zeros_like(below))
    above = jnp.where(coord < groups - 1, above, jnp.zeros_like(above))
    return jnp.concatenate([below, field, above], 1)


def faces(field):
    ends = {1: field.shape[2] - 1, -1: 0}
    endz = {1: field.shape[3] - 1, -1: 0}
    zf = jnp.stack([field[:, :, :, endz[d], :] for d in SIDES])
    yf = jnp.stack([field[:, :, ends[d], :, :] for d in SIDES])
    cf = jnp.stack([field[:, :, ends[dy], endz[dz], :] for dy in SIDES for dz in SIDES])
    return (zf, yf, cf)


def assemble(field, zf, yf, cf):
    mid = jnp.concatenate([zf[0][:, :, :, None], field, zf[1][:, :, :, None]], 3)
    rows = []
    for i in range(2):
        low, high = cf[2 * i][:, :, None, :], cf[2 * i + 1][:, :, None, :]
        rows.append(jnp.concatenate([low, yf[i], high], 2)[:, :, None])
    return jnp.concatenate([rows[0], mid, rows[1]], 2)


class Halo:
    def __init__(self, ins, outs, send, recv):
        me = lax.axis_index("space")
        self.me, self.send, self.recv = me, send, recv
        self.cz, self.cy = lax.rem(me, GZ), lax.rem(me // GZ, GY)
        self.src = [ins[k // 2].at[k % 2] if k < 4 else ins[2].at[k - 4] for k in range(8)]
        self.dst = [outs[k // 2].at[k % 2] if k < 4 else outs[2].at[k - 4] for k in range(8)]

    def has(self, dy, dz):
        y, z = self.cy + dy, self.cz + dz
        return (y >= 0) & (y < GY) & (z >= 0) & (z < GZ)

    def copy(self, k, to):
        return pltpu.make_async_remote_copy(
            src_ref=self.src[k],
            dst_ref=self.dst[k],
            send_sem=self.send.at[k],
            recv_sem=self.recv.at[k],
            device_id={"space": to},
            device_id_type=MESH,
        )

    def start(self):
        for k, (dy, dz) in enumerate(DIRS):

            @pl.when(self.has(dy, dz))
            def _():
                self.copy(k, self.me + dy * GZ + dz).start()

            @pl.when(jnp.logical_not(self.has(-dy, -dz)))
            def _():
                self.dst[k][...] = jnp.zeros(self.dst[k].shape, self.dst[k].dtype)

    def finish(self):
        for k, (dy, dz) in enumerate(DIRS):

            @pl.when(self.has(-dy, -dz))
            def _():
                self.copy(k, self.me).wait_recv()

            @pl.when(self.has(dy, dz))
            def _():
                self.copy(k, self.me).wait_send()


def greet(n, me, sample):
    barrier = pltpu.get_barrier_semaphore()

    def space_peer(d, _):
        pl.semaphore_signal(barrier, 1, device_id={"space": lax.rem(me + d, n)}, device_id_type=MESH)
        return 0

    lax.fori_loop(1, n, space_peer, 0)
    for d in range(1, 4):
        pl.semaphore_signal(barrier, 1, device_id={"sample": lax.rem(sample + d, 4)}, device_id_type=MESH)
    pl.semaphore_wait(barrier, n + 2)


def remote(src, dst, send, recv, **to):
    return pltpu.make_async_remote_copy(
        src_ref=src, dst_ref=dst, send_sem=send, recv_sem=recv, device_id=to, device_id_type=MESH
    )


LAG = 6


def gather_kernel(n, w, zi, yi, ci, out, zo, yo, co, hs, hr, as_, ar, bs, br, cs, cr):
    me, sample = lax.axis_index("space"), lax.axis_index("sample")
    core, x = lax.rem(sample, 2), sample // 2
    across, partner = (1 - x) * 2 + core, x * 2 + 1 - core
    greet(n, me, sample)
    halo = Halo((zi, yi, ci), (zo, yo, co), hs, hr)
    halo.start()

    def first(d, _):
        o = lax.rem(me + d, n)
        remote(w.at[core, x], out.at[me, core, x], as_.at[o], ar.at[me], space=o).start()
        return 0

    lax.fori_loop(1, n, first, 0)
    out[me] = w[...]

    def rest(t, _):
        @pl.when(t < n)
        def _():
            j = lax.rem(me - t + n, n)
            slot = out.at[j, core, x]
            remote(slot, slot, as_.at[j], ar.at[j], space=me).wait_recv()
            remote(slot, slot, bs.at[j], br.at[j], sample=across).start()

        @pl.when(t > LAG)
        def _():
            j = lax.rem(me - t + LAG + n, n)
            slot = out.at[j, core, 1 - x]
            remote(slot, slot, bs.at[j], br.at[j], sample=across).wait_recv()
            pair = out.at[j, core]
            remote(pair, pair, cs.at[j], cr.at[j], sample=partner).start()

        return 0

    lax.fori_loop(1, n + LAG, rest, 0)

    def last(d, _):
        o = lax.rem(me + d, n)
        pair = out.at[o, 1 - core]
        remote(pair, pair, cs.at[o], cr.at[o], sample=partner).wait_recv()
        remote(w.at[core, x], out.at[me, core, x], as_.at[o], ar.at[me], space=o).wait_send()
        slot = out.at[o, core, x]
        remote(slot, slot, bs.at[o], br.at[o], sample=across).wait_send()
        mine = out.at[o, core]
        remote(mine, mine, cs.at[o], cr.at[o], sample=partner).wait_send()
        return 0

    lax.fori_loop(1, n, last, 0)
    halo.finish()


def reduce_kernel(n, g, zi, yi, ci, out, zo, yo, co, r1, s2, r2, s3, r3, hs, hr, as_, ar, bs, br, cs, cr, ds, dr):
    me, sample = lax.axis_index("space"), lax.axis_index("sample")
    core, x = lax.rem(sample, 2), sample // 2
    across, partner = (1 - x) * 2 + core, x * 2 + 1 - core
    f32, bf16 = jnp.float32, jnp.bfloat16
    greet(n, me, sample)
    halo = Halo((zi, yi, ci), (zo, yo, co), hs, hr)
    halo.start()

    def owner(d):
        return lax.rem(me + 1 + d, n)

    def copy1(o):
        return remote(g.at[o, 1 - core], r1.at[o], as_.at[o], ar.at[o], sample=partner)

    def copy2(o):
        return remote(s2.at[o, 1 - x], r2.at[o], bs.at[o], br.at[o], sample=across)

    def copy3(o):
        return remote(s3.at[o], r3.at[me], cs.at[o], cr.at[me], space=o)

    def first(d, _):
        copy1(owner(d)).start()
        return 0

    lax.fori_loop(0, n, first, 0)

    def rest(t, _):
        @pl.when(t < n)
        def _():
            o = owner(t)
            copy1(o).wait_recv()
            s2[o] = (g[o, core].astype(f32) + r1[o].astype(f32)).astype(bf16)
            copy2(o).start()

        @pl.when(t >= LAG)
        def _():
            o = owner(t - LAG)
            copy2(o).wait_recv()
            s3[o] = (s2[o, x].astype(f32) + r2[o].astype(f32)).astype(bf16)

            @pl.when(t < n + LAG - 1)
            def _():
                copy3(o).start()

        return 0

    lax.fori_loop(0, n + LAG, rest, 0)

    def gather(d, total):
        j = lax.rem(me + n - d, n)
        remote(s3.at[j], r3.at[j], cs.at[j], cr.at[j], space=j).wait_recv()
        return total + r3[j].astype(f32)

    out[core, x] = lax.fori_loop(1, n, gather, s3[me].astype(f32))

    def copy4(d):
        mine = out.at[core, x]
        return remote(mine, mine, ds.at[d], dr.at[d], sample=lax.rem(sample + 1 + d, 4))

    for d in range(3):
        copy4(d).start()
    for d in range(3):
        copy4(d).wait()

    def drain(d, _):
        o = owner(d)
        copy1(o).wait_send()
        copy2(o).wait_send()

        @pl.when(d < n - 1)
        def _():
            copy3(o).wait_send()

        return 0

    lax.fori_loop(0, n, drain, 0)
    halo.finish()


def quarters(value, lead):
    rows = value.shape[-2]
    q = -(-rows // 4)
    if rows != 4 * q:
        value = jnp.pad(value, [(0, 0)] * (value.ndim - 2) + [(0, 4 * q - rows), (0, 0)])
    return value.reshape(*lead, 2, 2, q, value.shape[-1])


def whole_rows(value, rows):
    lead = value.shape[:-4]
    return value.reshape(*lead, -1, value.shape[-1])[..., :rows, :]


def like(arrays):
    return [jax.ShapeDtypeStruct(a.shape, a.dtype) for a in arrays]


def sems(*counts):
    return [pltpu.SemaphoreType.DMA((c,)) for c in counts]


def gather_weights(rows_bf, field):
    n = lax.axis_size("space")
    halo = faces(field)
    w = quarters(rows_bf, ())
    whole, zf, yf, cf = pl.pallas_call(
        functools.partial(gather_kernel, n),
        name="gather_and_halo",
        out_shape=[jax.ShapeDtypeStruct((n, *w.shape), w.dtype), *like(halo)],
        in_specs=[VM] * 4,
        out_specs=[VM] * 4,
        scratch_shapes=sems(8, 8, n, n, n, n, n, n),
        compiler_params=pltpu.CompilerParams(collective_id=0, has_side_effects=True),
    )(w, *halo)
    whole = whole_rows(whole, rows_bf.shape[0]).reshape(-1, rows_bf.shape[1])
    return whole, assemble(field, zf, yf, cf)


def reduce_grads(terms, rows, field):
    n = lax.axis_size("space")
    halo = faces(field)
    channels = terms.shape[-1]
    g = quarters(terms.reshape(n, rows, channels), (n,)).astype(jnp.bfloat16)
    q = g.shape[3]
    bf16 = jnp.bfloat16
    total, zf, yf, cf = pl.pallas_call(
        functools.partial(reduce_kernel, n),
        name="reduce_and_halo",
        out_shape=[jax.ShapeDtypeStruct((2, 2, q, channels), jnp.float32), *like(halo)],
        in_specs=[VM] * 4,
        out_specs=[VM] * 4,
        scratch_shapes=[
            pltpu.VMEM((n, 2, q, channels), bf16),
            pltpu.VMEM((n, 2, q, channels), bf16),
            pltpu.VMEM((n, q, channels), bf16),
            pltpu.VMEM((n, q, channels), bf16),
            pltpu.VMEM((n, q, channels), bf16),
            *sems(8, 8, n, n, n, n, n, n, 3, 3),
        ],
        compiler_params=pltpu.CompilerParams(collective_id=1, has_side_effects=True),
    )(g, *halo)
    return whole_rows(total, rows), assemble(field, zf, yf, cf)


def kernel_terms(padded, grad_pre):
    terms = lax.conv_general_dilated(
        padded,
        grad_pre,
        (1, 1, 1),
        "VALID",
        dimension_numbers=("CDHWN", "IDHWO", "DHWNC"),
        preferred_element_type=jnp.float32,
    )
    return terms.reshape(-1, terms.shape[-1])


def local(acts, weight, moment, second, cotangent):
    field = acts[:, 0]
    grad_out = cotangent[:, 0]
    channels = weight.shape[1]
    rows_bf = weight.astype(jnp.bfloat16)
    whole, padded = gather_weights(rows_bf, extend_x(field))
    kernel = whole.reshape(3, 3, 3, channels, channels)
    pre = convolve(padded, kernel)
    value, slope = activate(pre)
    output = value.astype(jnp.bfloat16)
    grad_pre = (grad_out.astype(jnp.float32) * slope).astype(jnp.bfloat16)
    flipped = jnp.flip(kernel, (0, 1, 2)).transpose(0, 1, 2, 4, 3)
    total = (
        field.shape[0]
        * lax.axis_size("sample")
        * lax.axis_size("space")
        * field.shape[1]
        * field.shape[2]
        * field.shape[3]
    )
    local_terms = kernel_terms(padded, grad_pre)
    summed, grad_padded = reduce_grads(local_terms, weight.shape[0], extend_x(grad_pre))
    input_grad = convolve(grad_padded, flipped).astype(jnp.bfloat16)
    weight_grad = summed * float(total) ** (-0.5)
    new_moment = 0.9 * moment + 0.1 * weight_grad
    new_second = 0.999 * second + 0.001 * weight_grad * weight_grad
    first_fix = 1.0 - 0.9**10
    second_fix = 1.0 - 0.999**10
    new_weight = weight - 0.001 * (new_moment / first_fix) / (
        jnp.sqrt(new_second / second_fix) + 1e-08
    )
    return (output[:, None], input_grad[:, None], weight_grad, new_weight, new_moment, new_second)


def solution(mesh):
    in_specs = (
        P("sample", "space", None, None, None, None),
        P("space", None),
        P("space", None),
        P("space", None),
        P("sample", "space", None, None, None, None),
    )
    out_specs = (
        P("sample", "space", None, None, None, None),
        P("sample", "space", None, None, None, None),
        P("space", None),
        P("space", None),
        P("space", None),
        P("space", None),
    )
    return jax.shard_map(local, mesh=mesh, in_specs=in_specs, out_specs=out_specs, check_vma=False)
```
